32 devices in a mesh: seq: 8 (over z, x), head: 4 (over y, core).
Axes of the slice: x: 2, y: 2, z: 4, core: 2. Of those that a mesh axis runs over, the one named last changes fastest.
Arguments:
- queries: bfloat16 [6144, 1536], P('seq', 'head'), may hold values from -24 to 24, as said below
- keys: bfloat16 [6144, 1536], P('seq', 'head'), may hold values from -24 to 24, as said below
- values: bfloat16 [6144, 1536], P('seq', 'head'), may hold values from -24 to 24
- learn_rate: float32 [4, 6144], P('head', 'seq'), may hold values from 0.02 to 0.5
- gate_fast: bfloat16 [4, 384, 384], P('head'), may hold values from -0.3125 to 0.3125
- up_fast: bfloat16 [4, 384, 384], P('head'), may hold values from -0.3125 to 0.3125
- down_fast: bfloat16 [4, 384, 384], P('head'), may hold values from -0.3125 to 0.3125
- ttt_gain: float32 [4, 384], P('head'), may hold values from 0.2 to 0.8
- out_weight: bfloat16 [1536, 1536], P('head'), may hold values from -0.15625 to 0.15625
Outputs:
- mixed: bfloat16 [6144, 1536], P('seq', 'head')
The draws below stay inside these ranges and needn't reach their ends.
Inputs may be any that keep to these rules, and one draw needn't show every extreme that they name: `queries`: real-valued activations. `keys`: real-valued activations.
All inputs are finite; a program needn't handle non-finite values.
Results may differ from the reference program's by a relative error of at most 0.014.
Values may be sent and summed in bfloat16 or wider, within the bound.
No kernel may reach another device: no remote copies, remote signals or barrier semaphores. Data moves between devices by JAX's collectives and lax.ppermute only.
A program may use at most 128 MiB of HBM per device.

```python
import math
import jax
import jax.numpy as jnp
from jax import lax

D = 1536
HEADS = 4
FH = 384
TOK_DEV = 768
HD = 384
WINDOW = 3072
TOKENS = 6144


def paired_rows(key):
    query_key = jax.random.fold_in(key, 11)
    key_key = jax.random.fold_in(key, 12)
    query_base = jax.random.normal(query_key, (TOKENS, D), jnp.float32)
    key_base = jax.random.normal(key_key, (TOKENS, D), jnp.float32)
    key_new = key_base
    query_new = query_base
    return (jnp.clip(query_new, -24.0, 24.0), jnp.clip(key_new, -24.0, 24.0))


def draw_queries(key, part):
    return paired_rows(key)[0].astype(jnp.bfloat16)


def draw_keys(key, part):
    return paired_rows(key)[1].astype(jnp.bfloat16)


def block_levels(key, dims, cuts, least, high):
    level = 1.0
    for position, blocks in cuts:
        draws = jax.random.uniform(jax.random.fold_in(jax.random.fold_in(key, 6), position), (blocks,), jnp.float32, least / len(cuts), high / len(cuts))
        level = level * jnp.repeat(jnp.exp(draws), dims[position] // blocks).reshape((-1,) + (1,) * (len(dims) - 1 - position))
    return level


def bell_draw(key, dims, spread, most, split=(), kind=jnp.bfloat16):
    level = block_levels(key, dims, split, -0.22, 0.18) if split else 1.0
    values = jax.random.normal(key, dims, jnp.float32) * spread * level
    return jnp.minimum(jnp.maximum(values, -most), most).astype(kind)


def setup_inputs(seed: int = 0) -> dict:
    streams_of = jax.random.split(jax.random.key(seed), 10)
    return {
        "queries": draw_queries(jax.random.fold_in(streams_of[9], 71), 0),
        "keys": draw_keys(jax.random.fold_in(streams_of[9], 71), 0),
        "values": bell_draw(streams_of[2], (TOKENS, D), 4.0, 24.0, ((0, 8), (1, 4))),
        "learn_rate": jnp.clip(jnp.exp(math.log(0.5) - 3.218876 * jax.random.uniform(streams_of[3], (HEADS, TOKENS), jnp.float32) ** block_levels(streams_of[3], (HEADS, TOKENS), ((0, 4), (1, 8)), -0.2, 0.2)), 0.02, 0.5),
        "gate_fast": bell_draw(streams_of[4], (HEADS, HD, FH), HD ** -0.5, 0.3125, ((0, 4),)),
        "up_fast": bell_draw(streams_of[5], (HEADS, HD, FH), HD ** -0.5, 0.3125, ((0, 4),)),
        "down_fast": bell_draw(streams_of[6], (HEADS, FH, HD), FH ** -0.5, 0.3125, ((0, 4),)),
        "ttt_gain": jnp.clip(0.2 + 0.6 * jax.random.uniform(streams_of[7], (HEADS, HD), jnp.float32) ** block_levels(streams_of[7], (HEADS, HD), ((0, 4),), -0.2, 0.2), 0.2, 0.8),
        "out_weight": bell_draw(streams_of[8], (D, D), D ** -0.5, 0.15625, ((0, 4),)),
    }


ns_first = 3.4445
ns_second = -4.775
ns_third = 2.0315
big_negative = -1e+30

def pair_scores(left, right):
    return lax.dot_general(left, right, (((1,), (1,)), ((), ())), preferred_element_type=jnp.float32)

def token_sum(left, right):
    return lax.dot_general(left, right, (((0,), (0,)), ((), ())), preferred_element_type=jnp.float32)

def orthogonalize(grad):
    current = grad / (jnp.sqrt(jnp.sum(grad * grad)) + 1e-07)
    for sweep in range(5):
        square = jnp.dot(current, current.T, precision=lax.Precision.HIGHEST)
        mixer = ns_second * square + ns_third * jnp.dot(square, square, precision=lax.Precision.HIGHEST)
        current = ns_first * current + jnp.dot(mixer, current, precision=lax.Precision.HIGHEST)
    return current

def attend_head(query_head, key_head, value_head):
    head_size = query_head.shape[1]
    scale = head_size ** (-0.5)
    key_pad = jnp.concatenate([jnp.zeros((WINDOW, head_size), key_head.dtype), key_head], axis=0)
    value_pad = jnp.concatenate([jnp.zeros((WINDOW, head_size), value_head.dtype), value_head], axis=0)
    count = TOKENS // TOK_DEV

    def one_block(block):
        start = (block * TOK_DEV).astype(jnp.int32)
        query_rows = lax.dynamic_slice_in_dim(query_head, start, TOK_DEV, 0)
        key_rows = lax.dynamic_slice_in_dim(key_pad, start, WINDOW + TOK_DEV, 0)
        value_rows = lax.dynamic_slice_in_dim(value_pad, start, WINDOW + TOK_DEV, 0)
        scores = pair_scores(query_rows, key_rows) * scale
        query_pos = start + jnp.arange(TOK_DEV, dtype=jnp.int32)
        key_pos = start - WINDOW + jnp.arange(WINDOW + TOK_DEV, dtype=jnp.int32)
        valid = (key_pos[None, :] <= query_pos[:, None]) & (key_pos[None, :] > query_pos[:, None] - WINDOW) & (key_pos[None, :] >= 0)
        scores = jnp.where(valid, scores, big_negative)
        top = lax.optimization_barrier(jnp.max(scores, axis=1, keepdims=True))
        expo = jnp.where(valid, jnp.exp(scores - top), 0.0)
        total = lax.optimization_barrier(jnp.sum(expo, axis=1, keepdims=True))
        weighted = jnp.dot(expo.astype(jnp.bfloat16), value_rows, preferred_element_type=jnp.float32)
        return weighted / total
    blocks = lax.map(one_block, jnp.arange(count, dtype=jnp.int32))
    return blocks.reshape(TOKENS, head_size)

def fast_branch(query_head, key_head, value_head, rate, gate_w, up_w, down_w, gain):
    gate_k = jnp.dot(key_head, gate_w, preferred_element_type=jnp.float32)
    up_k = jnp.dot(key_head, up_w, preferred_element_type=jnp.float32)
    sig = jax.nn.sigmoid(gate_k)
    hidden_k = (gate_k * sig * up_k).astype(jnp.bfloat16)
    target = (-rate[:, None] * value_head.astype(jnp.float32)).astype(jnp.bfloat16)
    grad_down = token_sum(hidden_k, target)
    back = pair_scores(target, down_w)
    grad_gate_k = (back * up_k * sig * (1.0 + gate_k * (1.0 - sig))).astype(jnp.bfloat16)
    grad_up_k = (back * gate_k * sig).astype(jnp.bfloat16)
    grad_gate = token_sum(key_head, grad_gate_k)
    grad_up = token_sum(key_head, grad_up_k)
    gate_new = (gate_w.astype(jnp.float32) - orthogonalize(grad_gate)).astype(jnp.bfloat16)
    up_new = (up_w.astype(jnp.float32) - orthogonalize(grad_up)).astype(jnp.bfloat16)
    down_new = (down_w.astype(jnp.float32) - orthogonalize(grad_down)).astype(jnp.bfloat16)
    query_gate = jnp.dot(query_head, gate_new, preferred_element_type=jnp.float32)
    query_up = jnp.dot(query_head, up_new, preferred_element_type=jnp.float32)
    query_hidden = (query_gate * jax.nn.sigmoid(query_gate) * query_up).astype(jnp.bfloat16)
    fast_out = jnp.dot(query_hidden, down_new, preferred_element_type=jnp.float32)
    normed = fast_out * lax.rsqrt(lax.optimization_barrier(jnp.mean(fast_out * fast_out, axis=1, keepdims=True)) + 1e-06)
    return normed * gain[None, :]

def reference(queries, keys, values, learn_rate, gate_fast, up_fast, down_fast, ttt_gain, out_weight):
    head_size = D // HEADS
    pieces = []
    for head in range(HEADS):
        cols = slice(head * head_size, (head + 1) * head_size)
        query_head = queries[:, cols]
        key_head = keys[:, cols]
        value_head = values[:, cols]
        attended = attend_head(query_head, key_head, value_head)
        fast = fast_branch(query_head, key_head, value_head, learn_rate[head], gate_fast[head], up_fast[head], down_fast[head], ttt_gain[head])
        pieces.append((attended + fast).astype(jnp.bfloat16))
    combined = jnp.concatenate(pieces, axis=1)
    return jnp.dot(combined, out_weight, preferred_element_type=jnp.float32).astype(jnp.bfloat16)
```

```python
import jax
import jax.numpy as jnp
from jax import lax
from jax.experimental import pallas as pl
from jax.experimental.pallas import tpu as pltpu
from jax.sharding import PartitionSpec as P

WIN_BLOCKS = 4
ROW_CHUNKS = 2
QUERY_TILES = 3

ns_first = 3.4445
ns_second = -4.775
ns_third = 2.0315
big_negative = -1e30

f32 = jnp.float32
bf16 = jnp.bfloat16


def dot(left, right):
    return lax.dot_general(left, right, (((1,), (0,)), ((), ())), preferred_element_type=f32)


def dot_rows(left, right):
    return lax.dot_general(left, right, (((1,), (1,)), ((), ())), preferred_element_type=f32)


def dot_tokens(left, right):
    return lax.dot_general(left, right, (((0,), (0,)), ((), ())), preferred_element_type=f32)


def swapped(shard, axis, mask):
    size = lax.axis_size(axis)
    return lax.ppermute(shard, axis, [(i, i ^ mask) for i in range(size)])


def shifted(shard, axis, by, keep=lambda i: True):
    size = lax.axis_size(axis)
    pairs = [(i, i + by) for i in range(size) if 0 <= i + by < size and keep(i)]
    return lax.ppermute(shard, axis, pairs)


def after(value, *others):
    return lax.optimization_barrier((value,) + others)[0]


def grad_body(side_ref, keys_ref, values_ref, rate_ref, gate_ref, up_ref, down_ref, keep_ref, send_ref):
    rows = keys_ref.shape[0]
    width = gate_ref.shape[1]
    tile = 128
    gate_w = gate_ref[...]
    up_w = up_ref[...]
    down_w = down_ref[...]
    sums = None
    step = 2 * tile if rows % (2 * tile) == 0 else tile
    for start in range(0, rows, step):
        k = keys_ref[start : start + step, :]
        v = values_ref[start : start + step, :]
        rate = jnp.concatenate(
            [
                jnp.transpose(
                    jnp.broadcast_to(rate_ref[:, s : s + tile], (tile, tile))
                )
                for s in range(start, start + step, tile)
            ],
            axis=0,
        )
        rate = jnp.concatenate([rate] * (v.shape[1] // tile), axis=1)
        gate_k = dot(k, gate_w)
        up_k = dot(k, up_w)
        sig = jax.nn.sigmoid(gate_k)
        hidden = (gate_k * sig * up_k).astype(bf16)
        target = (-rate * v.astype(f32)).astype(bf16)
        back = dot_rows(target, down_w)
        grad_gate = (back * up_k * sig * (1.0 + gate_k * (1.0 - sig))).astype(bf16)
        grad_up = (back * gate_k * sig).astype(bf16)
        part = (dot_tokens(k, grad_gate), dot_tokens(k, grad_up), dot_tokens(hidden, target))
        sums = part if sums is None else tuple(a + b for a, b in zip(sums, part))
    gate, up, down = sums
    half = down.shape[0] // 2
    side = side_ref[0] == 0
    rows_in = gate.shape[0]
    keep_ref[:rows_in, :] = jnp.where(side, gate, up)
    keep_ref[rows_in:, :] = jnp.where(side, down[:half], down[half:])
    send_ref[:rows_in, :] = jnp.where(side, up, gate).astype(bf16)
    send_ref[rows_in:, :] = jnp.where(side, down[half:], down[:half]).astype(bf16)


def whole(space=pltpu.VMEM):
    return pl.BlockSpec(memory_space=space)


def gradients(side, keys, values, rate, gate_w, up_w, down_w):
    shape = (gate_w.shape[0] + down_w.shape[0] // 2, gate_w.shape[1])
    return pl.pallas_call(
        grad_body,
        out_shape=(jax.ShapeDtypeStruct(shape, f32), jax.ShapeDtypeStruct(shape, bf16)),
        in_specs=[whole(pltpu.SMEM)] + [whole()] * 6,
        out_specs=(whole(), whole()),
        name="fast_gradients",
    )(side, keys, values, rate, gate_w, up_w, down_w)


def parts_of(x):
    high = x.astype(bf16)
    return high, (x - high.astype(f32)).astype(bf16)


def product(left, right, how):
    lh, ll = left
    rh, rl = right
    return how(lh, rh) + (how(lh, rl) + how(ll, rh))


def orthogonal(grad):
    current = grad / (jnp.sqrt(jnp.sum(grad * grad)) + 1e-07)
    for sweep in range(5):
        split = parts_of(current)
        square = product(split, split, dot_rows)
        pair = parts_of(square)
        mixer = ns_second * square + ns_third * product(pair, pair, dot)
        current = ns_first * current + product(parts_of(mixer), split, dot)
    return current


def single_body(side_ref, grad_ref, first_ref, second_ref, out_ref):
    weight = jnp.where(side_ref[0] == 0, first_ref[...].astype(f32), second_ref[...].astype(f32))
    out_ref[...] = (weight - orthogonal(grad_ref[...])).astype(bf16)


def single_update(side, grad, first, second):
    return pl.pallas_call(
        single_body,
        out_shape=jax.ShapeDtypeStruct(first.shape, bf16),
        in_specs=[whole(pltpu.SMEM)] + [whole()] * 3,
        out_specs=whole(),
        name="single_update",
    )(side, grad, first, second)


def joint_body(side_ref, mine_ref, other_ref, weight_ref, out_ref):
    mine = mine_ref[...]
    other = other_ref[...]
    side = side_ref[0] == 0
    grad = jnp.concatenate([jnp.where(side, mine, other), jnp.where(side, other, mine)], axis=0)
    out_ref[...] = (weight_ref[...].astype(f32) - orthogonal(grad)).astype(bf16)


def joint_update(side, mine, other, weight):
    return pl.pallas_call(
        joint_body,
        out_shape=jax.ShapeDtypeStruct(weight.shape, bf16),
        in_specs=[whole(pltpu.SMEM)] + [whole()] * 3,
        out_specs=whole(),
        name="joint_update",
    )(side, mine, other, weight)


def attend_body(kinds, first, flags_ref, q_ref, *refs):
    count = len(kinds)
    blocks = refs[:count]
    state = refs[count:]
    if first:
        top_ref, total_ref, acc_ref = state
    else:
        top_in, total_in, acc_in, top_ref, total_ref, acc_ref = state
        top_ref[...] = top_in[...]
        total_ref[...] = total_in[...]
        acc_ref[...] = acc_in[...]
    tile, size = q_ref.shape
    scale = size ** (-0.5)
    base = pl.program_id(0) * tile
    for at, (kind, block) in enumerate(zip(kinds, blocks)):

        def step(kind=kind, block=block):
            scores = dot_rows(q_ref[...], block[0]) * scale
            if kind != "full":
                row = base + lax.broadcasted_iota(jnp.int32, scores.shape, 0)
                col = lax.broadcasted_iota(jnp.int32, scores.shape, 1)
                scores = jnp.where(col <= row if kind == "own" else col > row, scores, big_negative)
            top = jnp.max(scores, axis=1, keepdims=True)
            if kind != "own":
                before = top_ref[:, :1]
                top = jnp.maximum(top, before)
                fade = jnp.exp(before - top)
            expo = jnp.exp(scores - top)
            total = jnp.sum(expo, axis=1, keepdims=True)
            moved = dot(expo.astype(bf16), block[1])
            if kind != "own":
                total = total + total_ref[:, :1] * fade
                moved = moved + acc_ref[...] * fade
            top_ref[...] = jnp.broadcast_to(top, top_ref.shape)
            total_ref[...] = jnp.broadcast_to(total, total_ref.shape)
            acc_ref[...] = moved

        if kind == "own":
            step()
        else:
            pl.when(flags_ref[at] != 0)(step)


def attend(flags, queries, kinds, blocks, state):
    rows, size = queries.shape
    tile = rows // QUERY_TILES
    thin = pl.BlockSpec((tile, 128), lambda i, s: (i, 0))
    wide = pl.BlockSpec((tile, size), lambda i, s: (i, 0))
    held = pl.BlockSpec(blocks[0].shape, lambda i, s: (0, 0, 0))
    first = state is None
    return pl.pallas_call(
        lambda *refs: attend_body(kinds, first, *refs),
        out_shape=(
            jax.ShapeDtypeStruct((rows, 128), f32),
            jax.ShapeDtypeStruct((rows, 128), f32),
            jax.ShapeDtypeStruct((rows, size), f32),
        ),
        grid_spec=pltpu.PrefetchScalarGridSpec(
            num_scalar_prefetch=1,
            grid=(QUERY_TILES,),
            in_specs=[wide] + [held] * len(blocks) + ([] if first else [thin, thin, wide]),
            out_specs=(thin, thin, wide),
        ),
        name="attend_" + "_".join(kinds),
    )(flags, queries, *blocks, *(() if first else state))


def fast_body(q_ref, gate_ref, up_ref, down_ref, gain_ref, total_ref, acc_ref, out_ref):
    q = q_ref[...]
    gate = dot(q, gate_ref[...])
    up = dot(q, up_ref[...])
    hidden = (gate * jax.nn.sigmoid(gate) * up).astype(bf16)
    fast = dot(hidden, down_ref[...])
    normed = fast * lax.rsqrt(jnp.mean(fast * fast, axis=1, keepdims=True) + 1e-06)
    attended = acc_ref[...] / total_ref[:, :1]
    out_ref[...] = (attended + normed * gain_ref[...]).astype(bf16)


def fast_rows(at, rows, queries, gate_w, up_w, down_w, gain, total, acc):
    size = queries.shape[1]
    spec = lambda width: pl.BlockSpec((rows, width), lambda i: (at, 0))
    held = lambda a: pl.BlockSpec(a.shape, lambda i: (0, 0))
    return pl.pallas_call(
        fast_body,
        out_shape=jax.ShapeDtypeStruct((rows, size), bf16),
        grid=(1,),
        in_specs=[spec(size), held(gate_w), held(up_w), held(down_w), held(gain), spec(128), spec(size)],
        out_specs=pl.BlockSpec((rows, size), lambda i: (0, 0)),
        name="fast_rows",
    )(queries, gate_w, up_w, down_w, gain, total, acc)


def project_body(*refs):
    count = (len(refs) - 1) // 2
    total = dot(refs[0][...], refs[count][...])
    for at in range(1, count):
        total = total + dot(refs[at][...], refs[count + at][...])
    refs[-1][...] = total.astype(bf16)


def project(shares, weights):
    return pl.pallas_call(
        project_body,
        out_shape=jax.ShapeDtypeStruct(shares[0].shape, bf16),
        in_specs=[whole()] * (2 * len(shares)),
        out_specs=whole(),
        name="project",
    )(*shares, *weights)


def window_blocks(stacked, block, size):
    odd = block % 2 == 1
    pair = swapped(stacked, "seq", 1)
    back_two = shifted(stacked, "seq", 2)
    crossed = shifted(pair, "seq", 2)
    if size == 2 * WIN_BLOCKS:
        steps = [(i, (i - 2) % size) for i in range(size - WIN_BLOCKS)]
        moved = lax.ppermute(stacked, "seq", steps)
        back_four = lax.ppermute(moved, "seq", [(j, (j - 2) % size) for _, j in steps])
    else:
        back_four = shifted(back_two, "seq", 2)
    across = shifted(back_four, "seq", -1, lambda i: i % 2 == 1)
    return [
        ("own", block >= 0, stacked),
        ("full", odd, pair),
        ("full", block >= 2, back_two),
        ("full", block >= 2, crossed),
        ("far", block >= 4, back_four),
        ("full", jnp.logical_and(block >= 4, jnp.logical_not(odd)), across),
    ]


def seq_masks(size):
    return 2, [1] + [(2 << k) - 2 for k in range(2, size.bit_length() - 1)]


def exchanged_columns(out_weight, head, heads):
    width = out_weight.shape[1] // heads
    shares = [lax.dynamic_slice_in_dim(out_weight, (head ^ o) * width, width, 1) for o in range(heads)]
    mask = heads // 2
    while mask:
        moving = [o for o in range(heads) if o & mask]
        got = swapped(jnp.stack([shares[o] for o in moving]), "head", mask)
        for at, o in enumerate(moving):
            shares[o] = got[at]
        mask //= 2
    return shares


def gathered_heads(share, heads):
    shares = {0: share}
    mask = heads // 2
    while mask:
        offsets = sorted(shares)
        got = swapped(jnp.stack([shares[o] for o in offsets]), "head", mask)
        for at, o in enumerate(offsets):
            shares[o ^ mask] = got[at]
        mask //= 2
    return [shares[o] for o in range(heads)]


def shards(queries, keys, values, learn_rate, gate_fast, up_fast, down_fast, ttt_gain, out_weight):
    size = lax.axis_size("seq")
    heads = lax.axis_size("head")
    block = lax.axis_index("seq")
    head = lax.axis_index("head")
    gate_w = gate_fast[0]
    up_w = up_fast[0]
    down_w = down_fast[0]
    side = ((block // 2 + block // 4) % 2).astype(jnp.int32).reshape(1)

    stacked = jnp.stack([keys, values])
    window = window_blocks(stacked, block, size)
    flags = jnp.stack([flag.astype(jnp.int32) for _, flag, _ in window])

    keep, send = gradients(side, keys, values, learn_rate, gate_w, up_w, down_w)
    halving, others = seq_masks(size)
    summed = keep + swapped(send, "seq", halving).astype(f32)
    for mask in others:
        summed = summed + swapped(summed.astype(bf16), "seq", mask).astype(f32)
    whole_rows = gate_w.shape[0]
    down_half = summed[whole_rows:]
    other_half = swapped(down_half, "seq", halving)
    mine_new = single_update(side, summed[:whole_rows], gate_w, up_w)
    other_new = swapped(mine_new, "seq", halving)
    down_new = joint_update(side, down_half, other_half, down_w)
    gate_new = jnp.where(side[0] == 0, mine_new, other_new)
    up_new = jnp.where(side[0] == 0, other_new, mine_new)

    state = None
    for lo, hi in ((0, 1), (1, 3), (3, 5), (5, 6)):
        picked = window[lo:hi]
        state = attend(
            flags[lo:hi], queries, tuple(kind for kind, _, _ in picked), [b for _, _, b in picked], state
        )
    top, total, acc = state

    weights = exchanged_columns(out_weight, head, heads)
    rows = queries.shape[0] // ROW_CHUNKS
    pieces = []
    for at in range(ROW_CHUNKS):
        share = fast_rows(at, rows, queries, gate_new, up_new, down_new, ttt_gain, total, acc)
        pieces.append(project(gathered_heads(share, heads), weights))
    return jnp.concatenate(pieces, axis=0)


def solution(mesh):
    placed = (
        P("seq", "head"),
        P("seq", "head"),
        P("seq", "head"),
        P("head", "seq"),
        P("head", None, None),
        P("head", None, None),
        P("head", None, None),
        P("head", None),
        P("head", None),
    )
    return jax.shard_map(
        shards, mesh=mesh, in_specs=placed, out_specs=P("seq", "head"), check_vma=False
    )
```
